32 devices in a mesh: seq: 8 (over z, x), head: 4 (over y, core).
Axes of the slice: x: 2, y: 2, z: 4, core: 2. Of those that a mesh axis runs over, the one named last changes fastest.
Arguments:
- queries: bfloat16 [2048, 1024], P('seq', 'head'), may hold values from -6 to 6
- key_rows: bfloat16 [2048, 1024], P('seq', 'head'), may hold values from -6 to 6
- value_rows: bfloat16 [2048, 1024], P('seq', 'head'), may hold values from -6 to 6
- out_weight: bfloat16 [1024, 1024], P('head'), may hold values from -0.1875 to 0.1875
- cotangent: bfloat16 [2048, 1024], P('seq'), may hold values from -6 to 6
Outputs:
- mixed_out: bfloat16 [2048, 1024], P(('seq', 'head'))
- query_grad: bfloat16 [2048, 1024], P('seq', 'head')
- key_grad: bfloat16 [2048, 1024], P('seq', 'head')
- value_grad: bfloat16 [2048, 1024], P('seq', 'head')
The draws below stay inside these ranges and needn't reach their ends.
All inputs are finite; a program needn't handle non-finite values.
Results may differ from the reference program's by a relative error of at most 0.023.
Values may be sent and summed in bfloat16 or wider, within the bound.
A program may use at most 64 MiB of HBM per device.

```python
import math
import jax
import jax.numpy as jnp
from jax import lax

D = 1024
HEAD_DIM = 64
FRAMES_DEV = 256
BLOCK = 128
POOL_ROWS = 64
FRAMES = 2048
N_SEQ = 8


def draw_both(key):
    query_key = jax.random.fold_in(key, 7001)
    keyrow_key = jax.random.fold_in(key, 7002)
    query_part = jnp.clip(2.0 * jax.random.normal(query_key, (FRAMES, D), dtype=jnp.float32), -6.0, 6.0)
    keyrow_part = jnp.clip(jax.random.normal(keyrow_key, (FRAMES, D), dtype=jnp.float32), -6.0, 6.0)
    return (query_part, keyrow_part)


def draw_queries(key, part):
    return draw_both(key)[0].astype(jnp.bfloat16)


def draw_key_rows(key, part):
    return draw_both(key)[1].astype(jnp.bfloat16)


def block_scale(stream_key, dims, split, low, high):
    loudness = 1.0
    for position, blocks in split:
        draws = jax.random.uniform(jax.random.fold_in(jax.random.fold_in(stream_key, 6), position), (blocks,), jnp.float32, low / len(split), high / len(split))
        loudness = loudness * jnp.repeat(jnp.exp(draws), dims[position] // blocks).reshape((-1,) + (1,) * (len(dims) - 1 - position))
    return loudness


def bell_draw(key, extent, width, bound, cuts=(), kind=jnp.bfloat16):
    level = block_scale(key, extent, cuts, -0.22, 0.18) if cuts else 1.0
    array = jax.random.normal(key, extent, jnp.float32) * width * level
    return jnp.minimum(jnp.maximum(array, -bound), bound).astype(kind)


def setup_inputs(seed: int = 0) -> dict:
    streams_of = jax.random.split(jax.random.key(seed), 6)
    return {
        "queries": draw_queries(jax.random.fold_in(streams_of[5], 71), 0),
        "key_rows": draw_key_rows(jax.random.fold_in(streams_of[5], 71), 0),
        "value_rows": bell_draw(streams_of[2], (FRAMES, D), 1.0, 6.0, ((0, 8), (1, 4))),
        "out_weight": bell_draw(streams_of[3], (D, D), D ** -0.5, 0.1875, ((0, 4),)),
        "cotangent": bell_draw(streams_of[4], (FRAMES, D), 1.0, 6.0, ((0, 8),)),
    }


masked_score = -1000000000.0

def rounded(tensor):
    return lax.optimization_barrier(tensor.astype(jnp.bfloat16)).astype(jnp.float32)

def attend(query_block, window_block, window_bias, coarse_rows):
    feature_width = query_block.shape[1]
    head_count = feature_width // HEAD_DIM
    blocks = query_block.shape[0] // BLOCK
    score_scale = 1.0 / math.sqrt(HEAD_DIM)
    query_tiles = rounded(query_block).reshape(blocks, BLOCK, head_count, HEAD_DIM)
    window_tiles = rounded(window_block).reshape(blocks + 2, BLOCK, 2 * feature_width)
    spread = jnp.concatenate([window_tiles[:-2], window_tiles[1:-1], window_tiles[2:]], axis=1)
    fine_keys = spread[:, :, :feature_width].reshape(blocks, 3 * BLOCK, head_count, HEAD_DIM)
    fine_values = spread[:, :, feature_width:].reshape(blocks, 3 * BLOCK, head_count, HEAD_DIM)
    bias_tiles = window_bias.reshape(blocks + 2, BLOCK)
    fine_bias = jnp.concatenate([bias_tiles[:-2], bias_tiles[1:-1], bias_tiles[2:]], axis=1)
    coarse_tiles = rounded(coarse_rows)
    coarse_keys = coarse_tiles[:, :feature_width].reshape(-1, head_count, HEAD_DIM)
    coarse_values = coarse_tiles[:, feature_width:].reshape(-1, head_count, HEAD_DIM)
    fine_scores = jnp.einsum('nqhd,nkhd->nhqk', query_tiles, fine_keys) * score_scale + fine_bias[:, None, None, :]
    coarse_scores = jnp.einsum('nqhd,khd->nhqk', query_tiles, coarse_keys) * score_scale
    row_max = lax.stop_gradient(jnp.maximum(fine_scores.max(axis=-1), coarse_scores.max(axis=-1)))[..., None]
    fine_exp = jnp.exp(fine_scores - row_max)
    coarse_exp = jnp.exp(coarse_scores - row_max)
    denominator = fine_exp.sum(axis=-1, keepdims=True) + coarse_exp.sum(axis=-1, keepdims=True)
    fine_weights = rounded(fine_exp / denominator)
    coarse_weights = rounded(coarse_exp / denominator)
    mixed_heads = jnp.einsum('nhqk,nkhd->nqhd', fine_weights, fine_values) + jnp.einsum('nhqk,khd->nqhd', coarse_weights, coarse_values)
    return mixed_heads.reshape(query_block.shape[0], feature_width).astype(jnp.bfloat16)

def local_attention(query_rows, window_rows, window_bias, coarse_rows):
    group_rows = math.gcd(query_rows.shape[0], 4 * BLOCK)
    group_total = query_rows.shape[0] // group_rows
    halo_rows = group_rows + 2 * BLOCK

    def one_group(group_index):
        first_row = group_index * group_rows
        return attend(lax.dynamic_slice_in_dim(query_rows, first_row, group_rows, 0), lax.dynamic_slice_in_dim(window_rows, first_row, halo_rows, 0), lax.dynamic_slice_in_dim(window_bias, first_row, halo_rows, 0), coarse_rows)
    pieces = lax.map(one_group, jnp.arange(group_total, dtype=jnp.int32))
    return pieces.reshape(query_rows.shape[0], query_rows.shape[1])

def pair_pool(panel):
    row_count = panel.shape[-2]
    paired = panel.reshape(panel.shape[:-2] + (row_count // 2, 2, panel.shape[-1]))
    return (paired[..., 0, :] + paired[..., 1, :]) / math.sqrt(2.0)

def panels_of(joined):
    pool_span = FRAMES_DEV // POOL_ROWS
    return joined.reshape(N_SEQ, POOL_ROWS, pool_span, joined.shape[1]).sum(axis=2) / math.sqrt(pool_span)

def coarse_sets(panel):
    feature_total = panel.shape[2]
    levels = [panel]
    current = panel
    bit_total = N_SEQ.bit_length() - 1
    for bit_index in range(bit_total):
        stride = 2 ** bit_index
        grouped = current.reshape(N_SEQ // (2 * stride), 2, stride, POOL_ROWS, feature_total)
        partner = grouped[:, ::-1].reshape(N_SEQ, POOL_ROWS, feature_total)
        levels.append(partner)
        merged = jnp.concatenate([pair_pool(grouped[:, 0]), pair_pool(grouped[:, 1])], axis=-2)
        current = jnp.broadcast_to(merged[:, None], grouped.shape).reshape(N_SEQ, POOL_ROWS, feature_total)
    return jnp.concatenate(levels, axis=1)

def reference(queries, key_rows, value_rows, out_weight, cotangent):

    def forward(query_all, key_all, value_all):
        joined = jnp.concatenate([key_all, value_all], axis=1)
        coarse = coarse_sets(panels_of(joined))
        padded = jnp.pad(joined, ((BLOCK, BLOCK), (0, 0)))
        positions = jnp.arange(FRAMES + 2 * BLOCK, dtype=jnp.int32) - BLOCK
        bias_all = jnp.where((positions >= 0) & (positions < FRAMES), 0.0, masked_score).astype(jnp.float32)

        def device_rows(device_index):
            first_row = device_index * FRAMES_DEV
            return local_attention(lax.dynamic_slice_in_dim(query_all, first_row, FRAMES_DEV, 0), lax.dynamic_slice_in_dim(padded, first_row, FRAMES_DEV + 2 * BLOCK, 0), lax.dynamic_slice_in_dim(bias_all, first_row, FRAMES_DEV + 2 * BLOCK, 0), lax.dynamic_index_in_dim(coarse, device_index, 0, keepdims=False))
        pieces = lax.map(device_rows, jnp.arange(N_SEQ, dtype=jnp.int32))
        return pieces.reshape(FRAMES, D)
    heads_out, pull = jax.vjp(forward, queries.astype(jnp.float32), key_rows.astype(jnp.float32), value_rows.astype(jnp.float32))
    mixed_out = jnp.dot(heads_out, out_weight, preferred_element_type=jnp.float32).astype(jnp.bfloat16)
    head_grad = jnp.dot(cotangent, out_weight.T, preferred_element_type=jnp.float32).astype(jnp.bfloat16)
    query_grad, key_grad, value_grad = pull(head_grad)
    return (mixed_out, query_grad.astype(jnp.bfloat16), key_grad.astype(jnp.bfloat16), value_grad.astype(jnp.bfloat16))
```

```python
import functools
import math

import jax
import jax.numpy as jnp
from jax import lax
from jax.experimental import pallas as pl
from jax.experimental.pallas import tpu as pltpu
from jax.sharding import PartitionSpec as P

HEAD_DIM = 64
PAIR = 2 * HEAD_DIM
BLOCK = 128
POOL_ROWS = 64
MIN_SLOT = 16
MASKED = -1000000000.0
MESH = pl.DeviceIdType.MESH
F32 = jnp.float32
BF16 = jnp.bfloat16


def dot_nn(a, b):
    return lax.dot_general(a, b, (((1,), (0,)), ((), ())), preferred_element_type=F32)


def dot_nt(a, b):
    return lax.dot_general(a, b, (((1,), (1,)), ((), ())), preferred_element_type=F32)


def dot_tn(a, b):
    return lax.dot_general(a, b, (((0,), (0,)), ((), ())), preferred_element_type=F32)


class Plan:
    def __init__(self, n_seq, frames):
        self.bits = n_seq.bit_length() - 1
        self.span = frames // POOL_ROWS
        self.rows = [POOL_ROWS >> b for b in range(self.bits)]
        self.slot = [max(MIN_SLOT, r) for r in self.rows]
        self.send_at, at = [], 0
        for b in range(self.bits):
            self.send_at.append(at)
            at += self.slot[b]
        self.send_rows = at
        self.coarse_rows = POOL_ROWS * (1 + self.bits)
        self.direct = [r >= MIN_SLOT for r in self.rows]
        self.wide_at, at = {}, 0
        for b in range(self.bits):
            if not self.direct[b]:
                self.wide_at[b] = at
                at += self.slot[b] << b
        self.wide_rows = max(at, MIN_SLOT)
        self.grad_at, at = {"own": 0}, POOL_ROWS
        for b in range(0, self.bits, 2):
            self.grad_at[b] = at
            at += self.slot[b] << b
        self.even_rows = at
        for b in range(1, self.bits, 2):
            self.grad_at[b] = at
            at += self.slot[b] << b
        self.grad_rows = at


def flip(me, m):
    out, b = me, 0
    while m >> b:
        if (m >> b) & 1:
            out = out + (1 << b) * (1 - 2 * (me // (1 << b) % 2))
        b += 1
    return out


def pool_matrix(plan, frames):
    row = lax.broadcasted_iota(jnp.int32, (plan.send_rows, frames), 0)
    col = lax.broadcasted_iota(jnp.int32, (plan.send_rows, frames), 1)
    hit = None
    for b in range(plan.bits):
        width = plan.span << b
        lo = plan.send_at[b]
        rel = col - (row - lo) * width
        now = (row >= lo) & (row < lo + plan.slot[b]) & (rel >= 0) & (rel < width)
        hit = now if hit is None else hit | now
    return jnp.where(hit, 1.0, 0.0).astype(BF16)


def spread_matrix(plan, frames, levels, base, width_all):
    frame = lax.broadcasted_iota(jnp.int32, (frames, width_all), 0)
    col = lax.broadcasted_iota(jnp.int32, (frames, width_all), 1)
    out = jnp.zeros((frames, width_all), F32)
    for level in levels:
        b = 0 if level == "own" else level
        lo = plan.grad_at[level] - base
        total = POOL_ROWS if level == "own" else plan.slot[b] << b
        width = plan.span << b
        rel = frame - ((col - lo) & (plan.slot[b] - 1)) * width
        hit = (col >= lo) & (col < lo + total) & (rel >= 0) & (rel < width)
        out = jnp.where(hit, 0.5 ** (b // 2), out)
    return out.astype(BF16)


def compact_matrix(plan, b):
    total = plan.slot[b] << b
    row = lax.broadcasted_iota(jnp.int32, (POOL_ROWS, total), 0)
    col = lax.broadcasted_iota(jnp.int32, (POOL_ROWS, total), 1)
    r = plan.rows[b]
    hit = ((col // plan.slot[b]) == (row // r)) & ((col & (plan.slot[b] - 1)) == (row & (r - 1)))
    return jnp.where(hit, 1.0, 0.0).astype(BF16)


def kernel(
    n_seq,
    n_head,
    plan,
    q_hbm,
    k_hbm,
    v_hbm,
    w_hbm,
    c_hbm,
    mixed_ref,
    qg_ref,
    kg_ref,
    vg_ref,
    q_ref,
    ext,
    w_ref,
    c_ref,
    pool_send,
    coarse,
    wide,
    hgrad,
    heads,
    qstack,
    gstack,
    weights,
    delta,
    mix_send,
    mix_recv,
    rim_send,
    rim_recv,
    inner,
    cg_send,
    grad,
    load_sem,
    halo_ssem,
    halo_rsem,
    pool_ssem,
    pool_rsem,
    rim_ssem,
    rim_rsem,
    cg_ssem,
    cg_rsem,
    mix_ssem,
    mix_rsem,
):
    me = lax.axis_index("seq")
    hme = lax.axis_index("head")
    frames, feats = q_ref.shape
    blocks = frames // BLOCK
    pairs = feats // PAIR
    bits = plan.bits
    window = 3 * BLOCK

    own_rows = pl.ds(BLOCK, frames)
    loads = [
        pltpu.make_async_copy(k_hbm, ext.at[own_rows, pl.ds(0, feats)], load_sem.at[0]),
        pltpu.make_async_copy(v_hbm, ext.at[own_rows, pl.ds(feats, feats)], load_sem.at[1]),
        pltpu.make_async_copy(c_hbm, c_ref, load_sem.at[2]),
        pltpu.make_async_copy(w_hbm, w_ref, load_sem.at[3]),
        pltpu.make_async_copy(q_hbm, q_ref, load_sem.at[4]),
    ]
    for load in loads:
        load.start()

    barrier = pltpu.get_barrier_semaphore()
    for m in range(1, n_seq):
        pl.semaphore_signal(barrier, inc=1, device_id=(flip(me, m), hme), device_id_type=MESH)
    for m in range(1, n_head):
        pl.semaphore_signal(
            barrier, inc=1, device_id=(me, lax.rem(hme + m, n_head)), device_id_type=MESH
        )

    @pl.when(me == 0)
    def _():
        ext[pl.ds(0, BLOCK), :] = jnp.zeros((BLOCK, 2 * feats), BF16)
        rim_recv[0] = jnp.zeros((BLOCK, 2 * feats), BF16)

    @pl.when(me == n_seq - 1)
    def _():
        ext[pl.ds(BLOCK + frames, BLOCK), :] = jnp.zeros((BLOCK, 2 * feats), BF16)
        rim_recv[1] = jnp.zeros((BLOCK, 2 * feats), BF16)

    loads[0].wait()
    loads[1].wait()
    sums = dot_nn(pool_matrix(plan, frames), ext[own_rows, :])
    for b in range(bits):
        at = plan.send_at[b]
        level = sums[at : at + plan.slot[b]] * (1.0 / math.sqrt(plan.span << b))
        pool_send[pl.ds(at, plan.slot[b]), :] = level.astype(BF16)
        if b == 0:
            coarse[pl.ds(0, POOL_ROWS), :] = level.astype(BF16)

    pl.semaphore_wait(barrier, n_seq - 1 + n_head - 1)

    def halo(side):
        return pltpu.make_async_remote_copy(
            src_ref=ext.at[pl.ds(frames if side == 0 else BLOCK, BLOCK), :],
            dst_ref=ext.at[pl.ds(0 if side == 0 else BLOCK + frames, BLOCK), :],
            send_sem=halo_ssem.at[side],
            recv_sem=halo_rsem.at[side],
            device_id=(me + 1 if side == 0 else me - 1, hme),
            device_id_type=MESH,
        )

    pool_copies = {}
    for m in reversed(range(1, n_seq)):
        b = m.bit_length() - 1
        slot = m - (1 << b)
        if plan.direct[b]:
            landing = coarse.at[pl.ds(POOL_ROWS * (1 + b) + slot * plan.slot[b], plan.slot[b]), :]
        else:
            landing = wide.at[pl.ds(plan.wide_at[b] + slot * plan.slot[b], plan.slot[b]), :]
        copy = pltpu.make_async_remote_copy(
            src_ref=pool_send.at[pl.ds(plan.send_at[b], plan.slot[b]), :],
            dst_ref=landing,
            send_sem=pool_ssem.at[m - 1],
            recv_sem=pool_rsem.at[m - 1],
            device_id=(flip(me, m), hme),
            device_id_type=MESH,
        )
        copy.start()
        pool_copies[m] = copy

    @pl.when(me < n_seq - 1)
    def _():
        halo(0).start()

    @pl.when(me > 0)
    def _():
        halo(1).start()

    loads[2].wait()
    loads[3].wait()
    hgrad[...] = dot_nt(c_ref[...], w_ref[...]).astype(BF16)
    loads[4].wait()

    lane = lax.broadcasted_iota(jnp.int32, (BLOCK, PAIR), 1)
    first = lane < HEAD_DIM

    def stacked(block):
        zero = jnp.zeros_like(block)
        return jnp.concatenate(
            [jnp.where(first, block, zero), jnp.where(first, zero, block)], axis=0
        )

    scale = 1.0 / math.sqrt(HEAD_DIM)
    for p in range(pairs):
        for n in range(blocks):
            u = p * blocks + n
            rows, cols = pl.ds(n * BLOCK, BLOCK), pl.ds(p * PAIR, PAIR)
            qstack[u] = (stacked(q_ref[rows, cols].astype(F32)) * scale).astype(BF16)
            gstack[u] = stacked(hgrad[rows, cols].astype(F32)).astype(BF16)

    for m in range(1, n_seq):
        pool_copies[m].wait()

    @pl.when(me > 0)
    def _():
        halo(0).wait_recv()
        halo(1).wait_send()

    @pl.when(me < n_seq - 1)
    def _():
        halo(1).wait_recv()
        halo(0).wait_send()

    for b in range(bits):
        if not plan.direct[b]:
            packed = wide[pl.ds(plan.wide_at[b], plan.slot[b] << b), :]
            coarse[pl.ds(POOL_ROWS * (1 + b), POOL_ROWS), :] = dot_nn(
                compact_matrix(plan, b), packed
            ).astype(BF16)

    left_bias = jnp.where(me == 0, MASKED, 0.0).astype(F32)
    right_bias = jnp.where(me == n_seq - 1, MASKED, 0.0).astype(F32)

    def keys(p, n, side):
        cols = pl.ds(side * feats + p * PAIR, PAIR)
        return ext[pl.ds(n * BLOCK, window), cols], coarse[:, cols]

    def heads_of(both):
        return jnp.concatenate(
            [both[:HEAD_DIM, :BLOCK], both[HEAD_DIM:, BLOCK:]], axis=0
        )

    for p in range(pairs):
        for n in range(blocks):
            u = p * blocks + n
            rows, cols = pl.ds(n * BLOCK, BLOCK), pl.ds(p * PAIR, PAIR)
            kf, kc = keys(p, n, 0)
            vf, vc = keys(p, n, 1)
            qs = qstack[u]
            sf = dot_nt(kf, qs)
            sc = dot_nt(kc, qs)
            parts = [sf[i * BLOCK : (i + 1) * BLOCK] for i in range(3)]
            if n == 0:
                parts[0] = parts[0] + left_bias
            if n == blocks - 1:
                parts[2] = parts[2] + right_bias
            parts.append(sc)
            top = functools.reduce(
                jnp.maximum, [x.max(axis=0, keepdims=True) for x in parts]
            )
            parts = [jnp.exp(x - top) for x in parts]
            total = sum(x.sum(axis=0, keepdims=True) for x in parts)
            inv = 1.0 / total
            parts = [(x * inv).astype(BF16) for x in parts]
            pf = jnp.concatenate(parts[:3], axis=0)
            pc = parts[3]
            weights[u, pl.ds(0, window), :] = pf
            weights[u, pl.ds(window, plan.coarse_rows), :] = pc
            out = heads_of(dot_tn(vf, pf) + dot_tn(vc, pc))
            heads[rows, cols] = out.T.astype(BF16)
            prod = out * hgrad[rows, cols].astype(F32).T
            delta[u] = jnp.concatenate(
                [
                    prod[:HEAD_DIM].sum(axis=0, keepdims=True),
                    prod[HEAD_DIM:].sum(axis=0, keepdims=True),
                ],
                axis=1,
            )

    share = frames // n_head
    mixed = dot_nn(heads[...], w_ref[...]).astype(BF16)
    for h in range(n_head):
        mix_send[h] = mixed[h * share : (h + 1) * share]
    mix_copies = []
    for m in range(1, n_head):
        peer = lax.rem(hme + m, n_head)
        copy = pltpu.make_async_remote_copy(
            src_ref=mix_send.at[peer],
            dst_ref=mix_recv.at[m - 1],
            send_sem=mix_ssem.at[m - 1],
            recv_sem=mix_rsem.at[m - 1],
            device_id=(me, peer),
            device_id_type=MESH,
        )
        copy.start()
        mix_copies.append(copy)

    for p in range(pairs):
        k_parts = [None] * (blocks + 2)
        v_parts = [None] * (blocks + 2)
        k_coarse = v_coarse = None
        for n in range(blocks):
            u = p * blocks + n
            rows, cols = pl.ds(n * BLOCK, BLOCK), pl.ds(p * PAIR, PAIR)
            kf, kc = keys(p, n, 0)
            vf, vc = keys(p, n, 1)
            qs, gs = qstack[u], gstack[u]
            pf = weights[u, pl.ds(0, window), :]
            pc = weights[u, pl.ds(window, plan.coarse_rows), :]
            dl = delta[u]
            df = (pf.astype(F32) * (dot_nt(vf, gs) - dl)).astype(BF16)
            dc = (pc.astype(F32) * (dot_nt(vc, gs) - dl)).astype(BF16)
            dvf, dvc = dot_nn(pf, gs), dot_nn(pc, gs)
            dkf, dkc = dot_nn(df, qs), dot_nn(dc, qs)
            dq = heads_of(dot_tn(kf, df) + dot_tn(kc, dc)) * scale
            qg_ref[rows, cols] = dq.T.astype(BF16)
            for i in range(3):
                piece = slice(i * BLOCK, (i + 1) * BLOCK)
                old = k_parts[n + i]
                k_parts[n + i] = dkf[piece] if old is None else old + dkf[piece]
                old = v_parts[n + i]
                v_parts[n + i] = dvf[piece] if old is None else old + dvf[piece]
            k_coarse = dkc if k_coarse is None else k_coarse + dkc
            v_coarse = dvc if v_coarse is None else v_coarse + dvc
        for side, fine, far in ((0, k_parts, k_coarse), (1, v_parts, v_coarse)):
            cols = pl.ds(side * feats + p * PAIR, PAIR)
            rim_send[0, :, cols] = fine[0].astype(BF16)
            rim_send[1, :, cols] = fine[-1].astype(BF16)
            for n in range(blocks):
                inner[pl.ds(n * BLOCK, BLOCK), cols] = fine[n + 1]
            far = far.astype(BF16)
            grad[pl.ds(0, POOL_ROWS), cols] = far[:POOL_ROWS]
            for b in range(bits):
                level = far[POOL_ROWS * (1 + b) : POOL_ROWS * (2 + b)]
                if not plan.direct[b]:
                    level = dot_tn(compact_matrix(plan, b), level).astype(BF16)
                at = plan.grad_at[b] - POOL_ROWS
                cg_send[pl.ds(at, plan.slot[b] << b), cols] = level

    cg_copies = {}
    for m in reversed(range(1, n_seq)):
        b = m.bit_length() - 1
        at = plan.grad_at[b] + (m - (1 << b)) * plan.slot[b]
        copy = pltpu.make_async_remote_copy(
            src_ref=cg_send.at[pl.ds(at - POOL_ROWS, plan.slot[b]), :],
            dst_ref=grad.at[pl.ds(at, plan.slot[b]), :],
            send_sem=cg_ssem.at[m - 1],
            recv_sem=cg_rsem.at[m - 1],
            device_id=(flip(me, m), hme),
            device_id_type=MESH,
        )
        copy.start()
        cg_copies[m] = copy

    def rim(side):
        return pltpu.make_async_remote_copy(
            src_ref=rim_send.at[side],
            dst_ref=rim_recv.at[1 - side],
            send_sem=rim_ssem.at[side],
            recv_sem=rim_rsem.at[side],
            device_id=(me - 1 if side == 0 else me + 1, hme),
            device_id_type=MESH,
        )

    @pl.when(me > 0)
    def _():
        rim(0).start()

    @pl.when(me < n_seq - 1)
    def _():
        rim(1).start()

    even = ["own"] + list(range(0, bits, 2))
    odd = list(range(1, bits, 2))
    even_t = spread_matrix(plan, frames, even, 0, plan.even_rows)
    if odd:
        odd_t = spread_matrix(
            plan, frames, odd, plan.even_rows, plan.grad_rows - plan.even_rows
        )

    for copy in mix_copies:
        copy.wait()
    acc = mix_send[hme].astype(F32)
    for m in range(1, n_head):
        acc = acc + mix_recv[m - 1].astype(F32)
    mixed_ref[...] = acc.astype(BF16)

    for m in range(1, n_seq):
        cg_copies[m].wait()
    root = 1.0 / math.sqrt(plan.span)
    total = inner[...] + dot_nn(even_t, grad[pl.ds(0, plan.even_rows), :]) * root
    if odd:
        total = total + dot_nn(
            odd_t, grad[pl.ds(plan.even_rows, plan.grad_rows - plan.even_rows), :]
        ) * (root / math.sqrt(2.0))
    inner[...] = total

    @pl.when(me > 0)
    def _():
        rim(1).wait_recv()
        rim(0).wait_send()

    @pl.when(me < n_seq - 1)
    def _():
        rim(0).wait_recv()
        rim(1).wait_send()

    head_rows, tail_rows = pl.ds(0, BLOCK), pl.ds(frames - BLOCK, BLOCK)
    inner[head_rows, :] = inner[head_rows, :] + rim_recv[0].astype(F32)
    inner[tail_rows, :] = inner[tail_rows, :] + rim_recv[1].astype(F32)
    kg_ref[...] = inner[:, :feats].astype(BF16)
    vg_ref[...] = inner[:, feats:].astype(BF16)


def body(queries, key_rows, value_rows, out_weight, cotangent):
    frames, feats = queries.shape
    width = out_weight.shape[1]
    n_seq, n_head = lax.axis_size("seq"), lax.axis_size("head")
    plan = Plan(n_seq, frames)
    units = (frames // BLOCK) * (feats // PAIR)
    keys = 3 * BLOCK + plan.coarse_rows
    share = frames // n_head
    dma = pltpu.SemaphoreType.DMA
    return pl.pallas_call(
        functools.partial(kernel, n_seq, n_head, plan),
        out_shape=(
            jax.ShapeDtypeStruct((share, width), BF16),
            jax.ShapeDtypeStruct((frames, feats), BF16),
            jax.ShapeDtypeStruct((frames, feats), BF16),
            jax.ShapeDtypeStruct((frames, feats), BF16),
        ),
        in_specs=[pl.BlockSpec(memory_space=pl.ANY)] * 5,
        out_specs=tuple([pl.BlockSpec(memory_space=pltpu.VMEM)] * 4),
        scratch_shapes=[
            pltpu.VMEM((frames, feats), BF16),
            pltpu.VMEM((frames + 2 * BLOCK, 2 * feats), BF16),
            pltpu.VMEM((feats, width), BF16),
            pltpu.VMEM((frames, width), BF16),
            pltpu.VMEM((plan.send_rows, 2 * feats), BF16),
            pltpu.VMEM((plan.coarse_rows, 2 * feats), BF16),
            pltpu.VMEM((plan.wide_rows, 2 * feats), BF16),
            pltpu.VMEM((frames, feats), BF16),
            pltpu.VMEM((frames, feats), BF16),
            pltpu.VMEM((units, 2 * BLOCK, PAIR), BF16),
            pltpu.VMEM((units, 2 * BLOCK, PAIR), BF16),
            pltpu.VMEM((units, keys, 2 * BLOCK), BF16),
            pltpu.VMEM((units, 1, 2 * BLOCK), F32),
            pltpu.VMEM((n_head, share, width), BF16),
            pltpu.VMEM((max(n_head - 1, 1), share, width), BF16),
            pltpu.VMEM((2, BLOCK, 2 * feats), BF16),
            pltpu.VMEM((2, BLOCK, 2 * feats), BF16),
            pltpu.VMEM((frames, 2 * feats), F32),
            pltpu.VMEM((plan.grad_rows - POOL_ROWS, 2 * feats), BF16),
            pltpu.VMEM((plan.grad_rows, 2 * feats), BF16),
            dma((5,)),
            dma((2,)),
            dma((2,)),
            dma((n_seq - 1,)),
            dma((n_seq - 1,)),
            dma((2,)),
            dma((2,)),
            dma((n_seq - 1,)),
            dma((n_seq - 1,)),
            dma((n_head - 1,)),
            dma((n_head - 1,)),
        ],
        compiler_params=pltpu.CompilerParams(
            collective_id=0, has_side_effects=True, vmem_limit_bytes=32 * 1024 * 1024
        ),
    )(queries, key_rows, value_rows, out_weight, cotangent)


def solution(mesh):
    placed = (P("seq", "head"), P("seq", "head"), P("seq", "head"), P("head", None), P("seq", None))
    return jax.shard_map(
        body,
        mesh=mesh,
        in_specs=placed,
        out_specs=(P(("seq", "head"), None), P("seq", "head"), P("seq", "head"), P("seq", "head")),
        check_vma=False,
    )
```

```python
import functools
import math

import jax
import jax.numpy as jnp
from jax import lax
from jax.experimental import pallas as pl
from jax.experimental.pallas import tpu as pltpu
from jax.sharding import PartitionSpec as P

HEAD_DIM = 64
PAIR = 2 * HEAD_DIM
BLOCK = 128
POOL_ROWS = 64
MIN_SLOT = 16
MASKED = -1000000000.0
MESH = pl.DeviceIdType.MESH
F32 = jnp.float32
BF16 = jnp.bfloat16


def dot_nn(a, b):
    return lax.dot_general(a, b, (((1,), (0,)), ((), ())), preferred_element_type=F32)


def dot_nt(a, b):
    return lax.dot_general(a, b, (((1,), (1,)), ((), ())), preferred_element_type=F32)


def dot_tn(a, b):
    return lax.dot_general(a, b, (((0,), (0,)), ((), ())), preferred_element_type=F32)


class Plan:
    def __init__(self, n_seq, frames):
        self.bits = n_seq.bit_length() - 1
        self.span = frames // POOL_ROWS
        self.rows = [POOL_ROWS >> b for b in range(self.bits)]
        self.slot = [max(MIN_SLOT, r) for r in self.rows]
        self.send_at, at = [], 0
        for b in range(self.bits):
            self.send_at.append(at)
            at += self.slot[b]
        self.send_rows = at
        self.coarse_rows = POOL_ROWS * (1 + self.bits)
        self.direct = [r >= MIN_SLOT for r in self.rows]
        self.wide_at, at = {}, 0
        for b in range(self.bits):
            if not self.direct[b]:
                self.wide_at[b] = at
                at += self.slot[b] << b
        self.wide_rows = max(at, MIN_SLOT)
        self.grad_at, at = {"own": 0}, POOL_ROWS
        for b in range(0, self.bits, 2):
            self.grad_at[b] = at
            at += self.slot[b] << b
        self.even_rows = at
        for b in range(1, self.bits, 2):
            self.grad_at[b] = at
            at += self.slot[b] << b
        self.grad_rows = at


def flip(me, m):
    out, b = me, 0
    while m >> b:
        if (m >> b) & 1:
            out = out + (1 << b) * (1 - 2 * (me // (1 << b) % 2))
        b += 1
    return out


def pool_matrix(plan, frames):
    row = lax.broadcasted_iota(jnp.int32, (plan.send_rows, frames), 0)
    col = lax.broadcasted_iota(jnp.int32, (plan.send_rows, frames), 1)
    hit = None
    for b in range(plan.bits):
        width = plan.span << b
        lo = plan.send_at[b]
        rel = col - (row - lo) * width
        now = (row >= lo) & (row < lo + plan.slot[b]) & (rel >= 0) & (rel < width)
        hit = now if hit is None else hit | now
    return jnp.where(hit, 1.0, 0.0).astype(BF16)


def spread_matrix(plan, frames, levels, base, width_all):
    frame = lax.broadcasted_iota(jnp.int32, (frames, width_all), 0)
    col = lax.broadcasted_iota(jnp.int32, (frames, width_all), 1)
    out = jnp.zeros((frames, width_all), F32)
    for level in levels:
        b = 0 if level == "own" else level
        lo = plan.grad_at[level] - base
        total = POOL_ROWS if level == "own" else plan.slot[b] << b
        width = plan.span << b
        rel = frame - ((col - lo) & (plan.slot[b] - 1)) * width
        hit = (col >= lo) & (col < lo + total) & (rel >= 0) & (rel < width)
        out = jnp.where(hit, 0.5 ** (b // 2), out)
    return out.astype(BF16)


def compact_matrix(plan, b):
    total = plan.slot[b] << b
    row = lax.broadcasted_iota(jnp.int32, (POOL_ROWS, total), 0)
    col = lax.broadcasted_iota(jnp.int32, (POOL_ROWS, total), 1)
    r = plan.rows[b]
    hit = ((col // plan.slot[b]) == (row // r)) & ((col & (plan.slot[b] - 1)) == (row & (r - 1)))
    return jnp.where(hit, 1.0, 0.0).astype(BF16)


def kernel(
    n_seq,
    n_head,
    plan,
    q_hbm,
    k_hbm,
    v_hbm,
    w_hbm,
    c_hbm,
    mixed_ref,
    qg_ref,
    kg_ref,
    vg_ref,
    q_ref,
    ext,
    w_ref,
    c_ref,
    pool_send,
    coarse,
    wide,
    hgrad,
    heads,
    qstack,
    gstack,
    weights,
    delta,
    mix_send,
    mix_recv,
    rim_send,
    rim_recv,
    inner,
    cg_send,
    grad,
    load_sem,
    halo_ssem,
    halo_rsem,
    pool_ssem,
    pool_rsem,
    rim_ssem,
    rim_rsem,
    cg_ssem,
    cg_rsem,
    mix_ssem,
    mix_rsem,
):
    me = lax.axis_index("seq")
    hme = lax.axis_index("head")
    frames, feats = q_ref.shape
    blocks = frames // BLOCK
    pairs = feats // PAIR
    bits = plan.bits
    window = 3 * BLOCK

    own_rows = pl.ds(BLOCK, frames)
    loads = [
        pltpu.make_async_copy(k_hbm, ext.at[own_rows, pl.ds(0, feats)], load_sem.at[0]),
        pltpu.make_async_copy(v_hbm, ext.at[own_rows, pl.ds(feats, feats)], load_sem.at[1]),
        pltpu.make_async_copy(c_hbm, c_ref, load_sem.at[2]),
        pltpu.make_async_copy(w_hbm, w_ref, load_sem.at[3]),
        pltpu.make_async_copy(q_hbm, q_ref, load_sem.at[4]),
    ]
    for load in loads:
        load.start()

    barrier = pltpu.get_barrier_semaphore()
    for m in range(1, n_seq):
        pl.semaphore_signal(barrier, inc=1, device_id=(flip(me, m), hme), device_id_type=MESH)
    for m in range(1, n_head):
        pl.semaphore_signal(
            barrier, inc=1, device_id=(me, lax.rem(hme + m, n_head)), device_id_type=MESH
        )

    @pl.when(me == 0)
    def _():
        ext[pl.ds(0, BLOCK), :] = jnp.zeros((BLOCK, 2 * feats), BF16)
        rim_recv[0] = jnp.zeros((BLOCK, 2 * feats), BF16)

    @pl.when(me == n_seq - 1)
    def _():
        ext[pl.ds(BLOCK + frames, BLOCK), :] = jnp.zeros((BLOCK, 2 * feats), BF16)
        rim_recv[1] = jnp.zeros((BLOCK, 2 * feats), BF16)

    loads[0].wait()
    loads[1].wait()
    sums = dot_nn(pool_matrix(plan, frames), ext[own_rows, :])
    for b in range(bits):
        at = plan.send_at[b]
        level = sums[at : at + plan.slot[b]] * (1.0 / math.sqrt(plan.span << b))
        pool_send[pl.ds(at, plan.slot[b]), :] = level.astype(BF16)
        if b == 0:
            coarse[pl.ds(0, POOL_ROWS), :] = level.astype(BF16)

    pl.semaphore_wait(barrier, n_seq - 1 + n_head - 1)

    def halo(side):
        return pltpu.make_async_remote_copy(
            src_ref=ext.at[pl.ds(frames if side == 0 else BLOCK, BLOCK), :],
            dst_ref=ext.at[pl.ds(0 if side == 0 else BLOCK + frames, BLOCK), :],
            send_sem=halo_ssem.at[side],
            recv_sem=halo_rsem.at[side],
            device_id=(me + 1 if side == 0 else me - 1, hme),
            device_id_type=MESH,
        )

    pool_copies = {}
    for m in reversed(range(1, n_seq)):
        b = m.bit_length() - 1
        slot = m - (1 << b)
        if plan.direct[b]:
            landing = coarse.at[pl.ds(POOL_ROWS * (1 + b) + slot * plan.slot[b], plan.slot[b]), :]
        else:
            landing = wide.at[pl.ds(plan.wide_at[b] + slot * plan.slot[b], plan.slot[b]), :]
        copy = pltpu.make_async_remote_copy(
            src_ref=pool_send.at[pl.ds(plan.send_at[b], plan.slot[b]), :],
            dst_ref=landing,
            send_sem=pool_ssem.at[m - 1],
            recv_sem=pool_rsem.at[m - 1],
            device_id=(flip(me, m), hme),
            device_id_type=MESH,
        )
        copy.start()
        pool_copies[m] = copy

    @pl.when(me < n_seq - 1)
    def _():
        halo(0).start()

    @pl.when(me > 0)
    def _():
        halo(1).start()

    loads[2].wait()
    loads[3].wait()
    hgrad[...] = dot_nt(c_ref[...], w_ref[...]).astype(BF16)
    loads[4].wait()

    lane = lax.broadcasted_iota(jnp.int32, (BLOCK, PAIR), 1)
    first = lane < HEAD_DIM

    def stacked(block):
        zero = jnp.zeros_like(block)
        return jnp.concatenate(
            [jnp.where(first, block, zero), jnp.where(first, zero, block)], axis=0
        )

    scale = 1.0 / math.sqrt(HEAD_DIM)
    for p in range(pairs):
        for n in range(blocks):
            u = p * blocks + n
            rows, cols = pl.ds(n * BLOCK, BLOCK), pl.ds(p * PAIR, PAIR)
            qstack[u] = (stacked(q_ref[rows, cols].astype(F32)) * scale).astype(BF16)
            gstack[u] = stacked(hgrad[rows, cols].astype(F32)).astype(BF16)

    for m in range(1, n_seq):
        pool_copies[m].wait()

    @pl.when(me > 0)
    def _():
        halo(0).wait_recv()
        halo(1).wait_send()

    @pl.when(me < n_seq - 1)
    def _():
        halo(1).wait_recv()
        halo(0).wait_send()

    for b in range(bits):
        if not plan.direct[b]:
            packed = wide[pl.ds(plan.wide_at[b], plan.slot[b] << b), :]
            coarse[pl.ds(POOL_ROWS * (1 + b), POOL_ROWS), :] = dot_nn(
                compact_matrix(plan, b), packed
            ).astype(BF16)

    left_bias = jnp.where(me == 0, MASKED, 0.0).astype(F32)
    right_bias = jnp.where(me == n_seq - 1, MASKED, 0.0).astype(F32)

    def keys(p, n, side):
        cols = pl.ds(side * feats + p * PAIR, PAIR)
        return ext[pl.ds(n * BLOCK, window), cols], coarse[:, cols]

    def heads_of(both):
        return jnp.concatenate(
            [both[:HEAD_DIM, :BLOCK], both[HEAD_DIM:, BLOCK:]], axis=0
        )

    for p in range(pairs):
        for n in range(blocks):
            u = p * blocks + n
            rows, cols = pl.ds(n * BLOCK, BLOCK), pl.ds(p * PAIR, PAIR)
            kf, kc = keys(p, n, 0)
            vf, vc = keys(p, n, 1)
            qs = qstack[u]
            sf = dot_nt(kf, qs)
            sc = dot_nt(kc, qs)
            parts = [sf[i * BLOCK : (i + 1) * BLOCK] for i in range(3)]
            if n == 0:
                parts[0] = parts[0] + left_bias
            if n == blocks - 1:
                parts[2] = parts[2] + right_bias
            parts.append(sc)
            top = functools.reduce(
                jnp.maximum, [x.max(axis=0, keepdims=True) for x in parts]
            )
            parts = [jnp.exp(x - top) for x in parts]
            total = sum(x.sum(axis=0, keepdims=True) for x in parts)
            inv = 1.0 / total
            parts = [(x * inv).astype(BF16) for x in parts]
            pf = jnp.concatenate(parts[:3], axis=0)
            pc = parts[3]
            weights[u, pl.ds(0, window), :] = pf
            weights[u, pl.ds(window, plan.coarse_rows), :] = pc
            out = heads_of(dot_tn(vf, pf) + dot_tn(vc, pc))
            heads[rows, cols] = out.T.astype(BF16)
            prod = out * hgrad[rows, cols].astype(F32).T
            delta[u] = jnp.concatenate(
                [
                    prod[:HEAD_DIM].sum(axis=0, keepdims=True),
                    prod[HEAD_DIM:].sum(axis=0, keepdims=True),
                ],
                axis=1,
            )

    share = frames // n_head
    mixed = dot_nn(heads[...], w_ref[...]).astype(BF16)
    for h in range(n_head):
        mix_send[h] = mixed[h * share : (h + 1) * share]
    mix_copies = []
    for m in range(1, n_head):
        peer = lax.rem(hme + m, n_head)
        copy = pltpu.make_async_remote_copy(
            src_ref=mix_send.at[peer],
            dst_ref=mix_recv.at[m - 1],
            send_sem=mix_ssem.at[m - 1],
            recv_sem=mix_rsem.at[m - 1],
            device_id=(me, peer),
            device_id_type=MESH,
        )
        copy.start()
        mix_copies.append(copy)

    for p in range(pairs):
        k_parts = [None] * (blocks + 2)
        v_parts = [None] * (blocks + 2)
        k_coarse = v_coarse = None
        for n in range(blocks):
            u = p * blocks + n
            rows, cols = pl.ds(n * BLOCK, BLOCK), pl.ds(p * PAIR, PAIR)
            kf, kc = keys(p, n, 0)
            vf, vc = keys(p, n, 1)
            qs, gs = qstack[u], gstack[u]
            pf = weights[u, pl.ds(0, window), :]
            pc = weights[u, pl.ds(window, plan.coarse_rows), :]
            dl = delta[u]
            df = (pf.astype(F32) * (dot_nt(vf, gs) - dl)).astype(BF16)
            dc = (pc.astype(F32) * (dot_nt(vc, gs) - dl)).astype(BF16)
            dvf, dvc = dot_nn(pf, gs), dot_nn(pc, gs)
            dkf, dkc = dot_nn(df, qs), dot_nn(dc, qs)
            dq = heads_of(dot_tn(kf, df) + dot_tn(kc, dc)) * scale
            qg_ref[rows, cols] = dq.T.astype(BF16)
            for i in range(3):
                piece = slice(i * BLOCK, (i + 1) * BLOCK)
                old = k_parts[n + i]
                k_parts[n + i] = dkf[piece] if old is None else old + dkf[piece]
                old = v_parts[n + i]
                v_parts[n + i] = dvf[piece] if old is None else old + dvf[piece]
            k_coarse = dkc if k_coarse is None else k_coarse + dkc
            v_coarse = dvc if v_coarse is None else v_coarse + dvc
        for side, fine, far in ((0, k_parts, k_coarse), (1, v_parts, v_coarse)):
            cols = pl.ds(side * feats + p * PAIR, PAIR)
            rim_send[0, :, cols] = fine[0].astype(BF16)
            rim_send[1, :, cols] = fine[-1].astype(BF16)
            for n in range(blocks):
                inner[pl.ds(n * BLOCK, BLOCK), cols] = fine[n + 1]
            far = far.astype(BF16)
            grad[pl.ds(0, POOL_ROWS), cols] = far[:POOL_ROWS]
            for b in range(bits):
                level = far[POOL_ROWS * (1 + b) : POOL_ROWS * (2 + b)]
                if not plan.direct[b]:
                    level = dot_tn(compact_matrix(plan, b), level).astype(BF16)
                at = plan.grad_at[b] - POOL_ROWS
                cg_send[pl.ds(at, plan.slot[b] << b), cols] = level

    cg_copies = {}
    for m in reversed(range(1, n_seq)):
        b = m.bit_length() - 1
        at = plan.grad_at[b] + (m - (1 << b)) * plan.slot[b]
        copy = pltpu.make_async_remote_copy(
            src_ref=cg_send.at[pl.ds(at - POOL_ROWS, plan.slot[b]), :],
            dst_ref=grad.at[pl.ds(at, plan.slot[b]), :],
            send_sem=cg_ssem.at[m - 1],
            recv_sem=cg_rsem.at[m - 1],
            device_id=(flip(me, m), hme),
            device_id_type=MESH,
        )
        copy.start()
        cg_copies[m] = copy

    def rim(side):
        return pltpu.make_async_remote_copy(
            src_ref=rim_send.at[side],
            dst_ref=rim_recv.at[1 - side],
            send_sem=rim_ssem.at[side],
            recv_sem=rim_rsem.at[side],
            device_id=(me - 1 if side == 0 else me + 1, hme),
            device_id_type=MESH,
        )

    @pl.when(me > 0)
    def _():
        rim(0).start()

    @pl.when(me < n_seq - 1)
    def _():
        rim(1).start()

    even = ["own"] + list(range(0, bits, 2))
    odd = list(range(1, bits, 2))
    even_t = spread_matrix(plan, frames, even, 0, plan.even_rows)
    if odd:
        odd_t = spread_matrix(
            plan, frames, odd, plan.even_rows, plan.grad_rows - plan.even_rows
        )

    for copy in mix_copies:
        copy.wait()
    acc = mix_send[hme].astype(F32)
    for m in range(1, n_head):
        acc = acc + mix_recv[m - 1].astype(F32)
    mixed_ref[...] = acc.astype(BF16)

    for m in range(1, n_seq):
        cg_copies[m].wait()
    root = 1.0 / math.sqrt(plan.span)
    total = inner[...] + dot_nn(even_t, grad[pl.ds(0, plan.even_rows), :]) * root
    if odd:
        total = total + dot_nn(
            odd_t, grad[pl.ds(plan.even_rows, plan.grad_rows - plan.even_rows), :]
        ) * (root / math.sqrt(2.0))
    inner[...] = total

    @pl.when(me > 0)
    def _():
        rim(1).wait_recv()
        rim(0).wait_send()

    @pl.when(me < n_seq - 1)
    def _():
        rim(0).wait_recv()
        rim(1).wait_send()

    head_rows, tail_rows = pl.ds(0, BLOCK), pl.ds(frames - BLOCK, BLOCK)
    inner[head_rows, :] = inner[head_rows, :] + rim_recv[0].astype(F32)
    inner[tail_rows, :] = inner[tail_rows, :] + rim_recv[1].astype(F32)
    kg_ref[...] = inner[:, :feats].astype(BF16)
    vg_ref[...] = inner[:, feats:].astype(BF16)


def put_out(a0, a1, a2, a3, b0, b1, b2, b3, sem):
    pairs = zip((a0, a1, a2, a3), (b0, b1, b2, b3))
    copies = [pltpu.make_async_copy(a, b, sem.at[i]) for i, (a, b) in enumerate(pairs)]
    for copy in copies:
        copy.start()
    for copy in copies:
        copy.wait()


def body(queries, key_rows, value_rows, out_weight, cotangent):
    frames, feats = queries.shape
    width = out_weight.shape[1]
    n_seq, n_head = lax.axis_size("seq"), lax.axis_size("head")
    plan = Plan(n_seq, frames)
    units = (frames // BLOCK) * (feats // PAIR)
    keys = 3 * BLOCK + plan.coarse_rows
    share = frames // n_head
    dma = pltpu.SemaphoreType.DMA
    operands = (queries, key_rows, value_rows, out_weight, cotangent)
    shapes = (
        jax.ShapeDtypeStruct((share, width), BF16),
        jax.ShapeDtypeStruct((frames, feats), BF16),
        jax.ShapeDtypeStruct((frames, feats), BF16),
        jax.ShapeDtypeStruct((frames, feats), BF16),
    )
    results = pl.pallas_call(
        functools.partial(kernel, n_seq, n_head, plan),
        out_shape=shapes,
        in_specs=[pl.BlockSpec(memory_space=pltpu.HBM)] * 5,
        out_specs=tuple([pl.BlockSpec(memory_space=pltpu.VMEM)] * 4),
        scratch_shapes=[
            pltpu.VMEM((frames, feats), BF16),
            pltpu.VMEM((frames + 2 * BLOCK, 2 * feats), BF16),
            pltpu.VMEM((feats, width), BF16),
            pltpu.VMEM((frames, width), BF16),
            pltpu.VMEM((plan.send_rows, 2 * feats), BF16),
            pltpu.VMEM((plan.coarse_rows, 2 * feats), BF16),
            pltpu.VMEM((plan.wide_rows, 2 * feats), BF16),
            pltpu.VMEM((frames, feats), BF16),
            pltpu.VMEM((frames, feats), BF16),
            pltpu.VMEM((units, 2 * BLOCK, PAIR), BF16),
            pltpu.VMEM((units, 2 * BLOCK, PAIR), BF16),
            pltpu.VMEM((units, keys, 2 * BLOCK), BF16),
            pltpu.VMEM((units, 1, 2 * BLOCK), F32),
            pltpu.VMEM((n_head, share, width), BF16),
            pltpu.VMEM((max(n_head - 1, 1), share, width), BF16),
            pltpu.VMEM((2, BLOCK, 2 * feats), BF16),
            pltpu.VMEM((2, BLOCK, 2 * feats), BF16),
            pltpu.VMEM((frames, 2 * feats), F32),
            pltpu.VMEM((plan.grad_rows - POOL_ROWS, 2 * feats), BF16),
            pltpu.VMEM((plan.grad_rows, 2 * feats), BF16),
            dma((5,)),
            dma((2,)),
            dma((2,)),
            dma((n_seq - 1,)),
            dma((n_seq - 1,)),
            dma((2,)),
            dma((2,)),
            dma((n_seq - 1,)),
            dma((n_seq - 1,)),
            dma((n_head - 1,)),
            dma((n_head - 1,)),
        ],
        compiler_params=pltpu.CompilerParams(
            collective_id=0, has_side_effects=True, vmem_limit_bytes=32 * 1024 * 1024
        ),
    )(*[pltpu.with_memory_space_constraint(x, pltpu.HBM) for x in operands])
    return pl.pallas_call(
        put_out,
        out_shape=shapes,
        in_specs=[pl.BlockSpec(memory_space=pl.ANY)] * 4,
        out_specs=tuple([pl.BlockSpec(memory_space=pltpu.HBM)] * 4),
        scratch_shapes=[dma((4,))],
        compiler_params=pltpu.CompilerParams(vmem_limit_bytes=1024 * 1024),
    )(*results)


def solution(mesh):
    placed = (P("seq", "head"), P("seq", "head"), P("seq", "head"), P("head", None), P("seq", None))
    return jax.shard_map(
        body,
        mesh=mesh,
        in_specs=placed,
        out_specs=(P(("seq", "head"), None), P("seq", "head"), P("seq", "head"), P("seq", "head")),
        check_vma=False,
    )
```

```python
import functools
import math

import jax
import jax.numpy as jnp
from jax import lax
from jax.experimental import pallas as pl
from jax.experimental.pallas import tpu as pltpu
from jax.sharding import PartitionSpec as P

HEAD_DIM = 64
PAIR = 2 * HEAD_DIM
BLOCK = 128
POOL_ROWS = 64
MIN_SLOT = 16
MASKED = -1000000000.0
MESH = pl.DeviceIdType.MESH
F32 = jnp.float32
BF16 = jnp.bfloat16


def dot_nn(a, b):
    return lax.dot_general(a, b, (((1,), (0,)), ((), ())), preferred_element_type=F32)


def dot_nt(a, b):
    return lax.dot_general(a, b, (((1,), (1,)), ((), ())), preferred_element_type=F32)


def dot_tn(a, b):
    return lax.dot_general(a, b, (((0,), (0,)), ((), ())), preferred_element_type=F32)


class Plan:
    def __init__(self, n_seq, frames):
        self.bits = n_seq.bit_length() - 1
        self.span = frames // POOL_ROWS
        self.rows = [POOL_ROWS >> b for b in range(self.bits)]
        self.slot = [max(MIN_SLOT, r) for r in self.rows]
        self.send_at, at = [], 0
        for b in range(self.bits):
            self.send_at.append(at)
            at += self.slot[b]
        self.send_rows = at
        self.coarse_rows = POOL_ROWS * (1 + self.bits)
        self.direct = [r >= MIN_SLOT for r in self.rows]
        self.wide_at, at = {}, 0
        for b in range(self.bits):
            if not self.direct[b]:
                self.wide_at[b] = at
                at += self.slot[b] << b
        self.wide_rows = max(at, MIN_SLOT)
        self.grad_at, at = {"own": 0}, POOL_ROWS
        for b in range(0, self.bits, 2):
            self.grad_at[b] = at
            at += self.slot[b] << b
        self.even_rows = at
        for b in range(1, self.bits, 2):
            self.grad_at[b] = at
            at += self.slot[b] << b
        self.grad_rows = at


def flip(me, m):
    out, b = me, 0
    while m >> b:
        if (m >> b) & 1:
            out = out + (1 << b) * (1 - 2 * (me // (1 << b) % 2))
        b += 1
    return out


def pool_matrix(plan, frames):
    row = lax.broadcasted_iota(jnp.int32, (plan.send_rows, frames), 0)
    col = lax.broadcasted_iota(jnp.int32, (plan.send_rows, frames), 1)
    hit = None
    for b in range(plan.bits):
        width = plan.span << b
        lo = plan.send_at[b]
        rel = col - (row - lo) * width
        now = (row >= lo) & (row < lo + plan.slot[b]) & (rel >= 0) & (rel < width)
        hit = now if hit is None else hit | now
    return jnp.where(hit, 1.0, 0.0).astype(BF16)


def spread_matrix(plan, frames, levels, base, width_all):
    frame = lax.broadcasted_iota(jnp.int32, (frames, width_all), 0)
    col = lax.broadcasted_iota(jnp.int32, (frames, width_all), 1)
    out = jnp.zeros((frames, width_all), F32)
    for level in levels:
        b = 0 if level == "own" else level
        lo = plan.grad_at[level] - base
        total = POOL_ROWS if level == "own" else plan.slot[b] << b
        width = plan.span << b
        rel = frame - ((col - lo) & (plan.slot[b] - 1)) * width
        hit = (col >= lo) & (col < lo + total) & (rel >= 0) & (rel < width)
        out = jnp.where(hit, 0.5 ** (b // 2), out)
    return out.astype(BF16)


def compact_matrix(plan, b):
    total = plan.slot[b] << b
    row = lax.broadcasted_iota(jnp.int32, (POOL_ROWS, total), 0)
    col = lax.broadcasted_iota(jnp.int32, (POOL_ROWS, total), 1)
    r = plan.rows[b]
    hit = ((col // plan.slot[b]) == (row // r)) & ((col & (plan.slot[b] - 1)) == (row & (r - 1)))
    return jnp.where(hit, 1.0, 0.0).astype(BF16)


def kernel(
    n_seq,
    n_head,
    plan,
    q_hbm,
    k_hbm,
    v_hbm,
    w_hbm,
    c_hbm,
    mixed_ref,
    qg_ref,
    kg_ref,
    vg_ref,
    q_ref,
    ext,
    w_ref,
    c_ref,
    pool_send,
    coarse,
    wide,
    hgrad,
    heads,
    qstack,
    gstack,
    weights,
    delta,
    mix_send,
    mix_recv,
    rim_send,
    rim_recv,
    inner,
    cg_send,
    grad,
    spread,
    load_sem,
    halo_ssem,
    halo_rsem,
    pool_ssem,
    pool_rsem,
    rim_ssem,
    rim_rsem,
    cg_ssem,
    cg_rsem,
    mix_ssem,
    mix_rsem,
):
    me = lax.axis_index("seq")
    hme = lax.axis_index("head")
    frames, feats = q_ref.shape
    blocks = frames // BLOCK
    pairs = feats // PAIR
    bits = plan.bits
    window = 3 * BLOCK
    peers = n_seq - 1

    own_rows = pl.ds(BLOCK, frames)
    k_cols, v_cols = pl.ds(0, PAIR), pl.ds(PAIR, PAIR)
    loads = []
    for p in range(pairs):
        cols = pl.ds(p * PAIR, PAIR)
        for side, (hbm, to) in enumerate(((k_hbm, k_cols), (v_hbm, v_cols))):
            loads.append(
                pltpu.make_async_copy(
                    hbm.at[:, cols], ext.at[p, own_rows, to], load_sem.at[2 * p + side]
                )
            )
    for i, (hbm, ref) in enumerate(((c_hbm, c_ref), (w_hbm, w_ref), (q_hbm, q_ref))):
        loads.append(pltpu.make_async_copy(hbm, ref, load_sem.at[2 * pairs + i]))
    for load in loads:
        load.start()

    barrier = pltpu.get_barrier_semaphore()
    for m in reversed(range(1, n_seq)):
        pl.semaphore_signal(barrier, inc=1, device_id=(flip(me, m), hme), device_id_type=MESH)
    for m in range(1, n_head):
        pl.semaphore_signal(
            barrier, inc=1, device_id=(me, lax.rem(hme + m, n_head)), device_id_type=MESH
        )

    @pl.when(me == 0)
    def _():
        for p in range(pairs):
            ext[p, pl.ds(0, BLOCK), :] = jnp.zeros((BLOCK, 2 * PAIR), BF16)
            rim_recv[p, 0] = jnp.zeros((BLOCK, 2 * PAIR), BF16)

    @pl.when(me == n_seq - 1)
    def _():
        for p in range(pairs):
            ext[p, pl.ds(BLOCK + frames, BLOCK), :] = jnp.zeros((BLOCK, 2 * PAIR), BF16)
            rim_recv[p, 1] = jnp.zeros((BLOCK, 2 * PAIR), BF16)

    pooling = pool_matrix(plan, frames)
    for p in range(pairs):
        loads[2 * p].wait()
        loads[2 * p + 1].wait()
        sums = dot_nn(pooling, ext[p, own_rows, :])
        for b in range(bits):
            at = plan.send_at[b]
            level = sums[at : at + plan.slot[b]] * (1.0 / math.sqrt(plan.span << b))
            pool_send[p, pl.ds(at, plan.slot[b]), :] = level.astype(BF16)
            if b == 0:
                coarse[p, pl.ds(0, POOL_ROWS), :] = level.astype(BF16)

    def halo(p, side):
        return pltpu.make_async_remote_copy(
            src_ref=ext.at[p, pl.ds(frames if side == 0 else BLOCK, BLOCK), :],
            dst_ref=ext.at[p, pl.ds(0 if side == 0 else BLOCK + frames, BLOCK), :],
            send_sem=halo_ssem.at[2 * p + side],
            recv_sem=halo_rsem.at[2 * p + side],
            device_id=(me + 1 if side == 0 else me - 1, hme),
            device_id_type=MESH,
        )

    def panel(p, m):
        b = m.bit_length() - 1
        slot = m - (1 << b)
        if plan.direct[b]:
            at = POOL_ROWS * (1 + b) + slot * plan.slot[b]
            landing = coarse.at[p, pl.ds(at, plan.slot[b]), :]
        else:
            at = plan.wide_at[b] + slot * plan.slot[b]
            landing = wide.at[p, pl.ds(at, plan.slot[b]), :]
        return pltpu.make_async_remote_copy(
            src_ref=pool_send.at[p, pl.ds(plan.send_at[b], plan.slot[b]), :],
            dst_ref=landing,
            send_sem=pool_ssem.at[p * peers + m - 1],
            recv_sem=pool_rsem.at[p * peers + m - 1],
            device_id=(flip(me, m), hme),
            device_id_type=MESH,
        )

    def far_grad(p, m):
        b = m.bit_length() - 1
        at = plan.grad_at[b] + (m - (1 << b)) * plan.slot[b]
        return pltpu.make_async_remote_copy(
            src_ref=cg_send.at[p, pl.ds(at - POOL_ROWS, plan.slot[b]), :],
            dst_ref=grad.at[p, pl.ds(at, plan.slot[b]), :],
            send_sem=cg_ssem.at[p * peers + m - 1],
            recv_sem=cg_rsem.at[p * peers + m - 1],
            device_id=(flip(me, m), hme),
            device_id_type=MESH,
        )

    def rim(p, side):
        return pltpu.make_async_remote_copy(
            src_ref=rim_send.at[p, side],
            dst_ref=rim_recv.at[p, 1 - side],
            send_sem=rim_ssem.at[2 * p + side],
            recv_sem=rim_rsem.at[2 * p + side],
            device_id=(me - 1 if side == 0 else me + 1, hme),
            device_id_type=MESH,
        )

    pl.semaphore_wait(barrier, n_seq - 1 + n_head - 1)

    for p in range(pairs):
        for m in reversed(range(1, n_seq)):
            panel(p, m).start()

        @pl.when(me < n_seq - 1)
        def _():
            halo(p, 0).start()

        @pl.when(me > 0)
        def _():
            halo(p, 1).start()

    for load in loads[2 * pairs :]:
        load.wait()
    hgrad[...] = dot_nt(c_ref[...], w_ref[...]).astype(BF16)

    lane = lax.broadcasted_iota(jnp.int32, (BLOCK, PAIR), 1)
    first = lane < HEAD_DIM

    def stacked(block):
        zero = jnp.zeros_like(block)
        return jnp.concatenate(
            [jnp.where(first, block, zero), jnp.where(first, zero, block)], axis=0
        )

    scale = 1.0 / math.sqrt(HEAD_DIM)
    for p in range(pairs):
        for n in range(blocks):
            u = p * blocks + n
            rows, cols = pl.ds(n * BLOCK, BLOCK), pl.ds(p * PAIR, PAIR)
            qstack[u] = (stacked(q_ref[rows, cols].astype(F32)) * scale).astype(BF16)
            gstack[u] = stacked(hgrad[rows, cols].astype(F32)).astype(BF16)

    even = ["own"] + list(range(0, bits, 2))
    odd = list(range(1, bits, 2))
    spread[:, pl.ds(0, plan.even_rows)] = spread_matrix(plan, frames, even, 0, plan.even_rows)
    odd_rows = plan.grad_rows - plan.even_rows
    if odd:
        spread[:, pl.ds(plan.even_rows, odd_rows)] = spread_matrix(
            plan, frames, odd, plan.even_rows, odd_rows
        )

    left_bias = jnp.where(me == 0, MASKED, 0.0).astype(F32)
    right_bias = jnp.where(me == n_seq - 1, MASKED, 0.0).astype(F32)

    def keys(p, n, cols):
        return ext[p, pl.ds(n * BLOCK, window), cols], coarse[p, :, cols]

    def heads_of(both):
        return jnp.concatenate([both[:HEAD_DIM, :BLOCK], both[HEAD_DIM:, BLOCK:]], axis=0)

    def arrive(p):
        for m in range(1, n_seq):
            panel(p, m).wait()

        @pl.when(me > 0)
        def _():
            halo(p, 0).wait_recv()
            halo(p, 1).wait_send()

        @pl.when(me < n_seq - 1)
        def _():
            halo(p, 1).wait_recv()
            halo(p, 0).wait_send()

        for b in range(bits):
            if not plan.direct[b]:
                packed = wide[p, pl.ds(plan.wide_at[b], plan.slot[b] << b), :]
                coarse[p, pl.ds(POOL_ROWS * (1 + b), POOL_ROWS), :] = dot_nn(
                    compact_matrix(plan, b), packed
                ).astype(BF16)

    def forward(p):
        for n in range(blocks):
            u = p * blocks + n
            rows, cols = pl.ds(n * BLOCK, BLOCK), pl.ds(p * PAIR, PAIR)
            kf, kc = keys(p, n, k_cols)
            vf, vc = keys(p, n, v_cols)
            qs = qstack[u]
            sf = dot_nt(kf, qs)
            sc = dot_nt(kc, qs)
            parts = [sf[i * BLOCK : (i + 1) * BLOCK] for i in range(3)]
            if n == 0:
                parts[0] = parts[0] + left_bias
            if n == blocks - 1:
                parts[2] = parts[2] + right_bias
            parts.append(sc)
            top = functools.reduce(jnp.maximum, [x.max(axis=0, keepdims=True) for x in parts])
            parts = [jnp.exp(x - top) for x in parts]
            total = sum(x.sum(axis=0, keepdims=True) for x in parts)
            inv = 1.0 / total
            parts = [(x * inv).astype(BF16) for x in parts]
            pf = jnp.concatenate(parts[:3], axis=0)
            pc = parts[3]
            weights[u, pl.ds(0, window), :] = pf
            weights[u, pl.ds(window, plan.coarse_rows), :] = pc
            out = heads_of(dot_tn(vf, pf) + dot_tn(vc, pc))
            heads[rows, cols] = out.T.astype(BF16)
            prod = out * hgrad[rows, cols].astype(F32).T
            delta[u] = jnp.concatenate(
                [
                    prod[:HEAD_DIM].sum(axis=0, keepdims=True),
                    prod[HEAD_DIM:].sum(axis=0, keepdims=True),
                ],
                axis=1,
            )

    def backward(p):
        k_parts = [None] * (blocks + 2)
        v_parts = [None] * (blocks + 2)
        k_coarse = v_coarse = None
        for n in range(blocks):
            u = p * blocks + n
            rows, cols = pl.ds(n * BLOCK, BLOCK), pl.ds(p * PAIR, PAIR)
            kf, kc = keys(p, n, k_cols)
            vf, vc = keys(p, n, v_cols)
            qs, gs = qstack[u], gstack[u]
            pf = weights[u, pl.ds(0, window), :]
            pc = weights[u, pl.ds(window, plan.coarse_rows), :]
            dl = delta[u]
            df = (pf.astype(F32) * (dot_nt(vf, gs) - dl)).astype(BF16)
            dc = (pc.astype(F32) * (dot_nt(vc, gs) - dl)).astype(BF16)
            dvf, dvc = dot_nn(pf, gs), dot_nn(pc, gs)
            dkf, dkc = dot_nn(df, qs), dot_nn(dc, qs)
            dq = heads_of(dot_tn(kf, df) + dot_tn(kc, dc)) * scale
            qg_ref[rows, cols] = dq.T.astype(BF16)
            for i in range(3):
                piece = slice(i * BLOCK, (i + 1) * BLOCK)
                old = k_parts[n + i]
                k_parts[n + i] = dkf[piece] if old is None else old + dkf[piece]
                old = v_parts[n + i]
                v_parts[n + i] = dvf[piece] if old is None else old + dvf[piece]
            k_coarse = dkc if k_coarse is None else k_coarse + dkc
            v_coarse = dvc if v_coarse is None else v_coarse + dvc
        for fine, far, cols in ((k_parts, k_coarse, k_cols), (v_parts, v_coarse, v_cols)):
            rim_send[p, 0, :, cols] = fine[0].astype(BF16)
            rim_send[p, 1, :, cols] = fine[-1].astype(BF16)
            for n in range(blocks):
                inner[p, pl.ds(n * BLOCK, BLOCK), cols] = fine[n + 1]
            far = far.astype(BF16)
            grad[p, pl.ds(0, POOL_ROWS), cols] = far[:POOL_ROWS]
            for b in range(bits):
                level = far[POOL_ROWS * (1 + b) : POOL_ROWS * (2 + b)]
                if not plan.direct[b]:
                    level = dot_tn(compact_matrix(plan, b), level).astype(BF16)
                at = plan.grad_at[b] - POOL_ROWS
                cg_send[p, pl.ds(at, plan.slot[b] << b), cols] = level

        for m in reversed(range(1, n_seq)):
            far_grad(p, m).start()

        @pl.when(me > 0)
        def _():
            rim(p, 0).start()

        @pl.when(me < n_seq - 1)
        def _():
            rim(p, 1).start()

    share = frames // n_head

    def mix(m):
        peer = lax.rem(hme + m, n_head)
        return pltpu.make_async_remote_copy(
            src_ref=mix_send.at[peer],
            dst_ref=mix_recv.at[m - 1],
            send_sem=mix_ssem.at[m - 1],
            recv_sem=mix_rsem.at[m - 1],
            device_id=(me, peer),
            device_id_type=MESH,
        )

    for p in range(pairs):
        arrive(p)
        forward(p)
        if p == pairs - 1:
            mixed = dot_nn(heads[...], w_ref[...]).astype(BF16)
            for h in range(n_head):
                mix_send[h] = mixed[h * share : (h + 1) * share]
            for m in range(1, n_head):
                mix(m).start()
        backward(p)

    root = 1.0 / math.sqrt(plan.span)
    head_rows, tail_rows = pl.ds(0, BLOCK), pl.ds(frames - BLOCK, BLOCK)

    def collect(p):
        for m in range(1, n_seq):
            far_grad(p, m).wait()
        total = inner[p] + root * dot_nn(
            spread[:, pl.ds(0, plan.even_rows)], grad[p, pl.ds(0, plan.even_rows), :]
        )
        if odd:
            total = total + (root / math.sqrt(2.0)) * dot_nn(
                spread[:, pl.ds(plan.even_rows, odd_rows)],
                grad[p, pl.ds(plan.even_rows, odd_rows), :],
            )
        inner[p] = total

        @pl.when(me > 0)
        def _():
            rim(p, 1).wait_recv()
            rim(p, 0).wait_send()

        @pl.when(me < n_seq - 1)
        def _():
            rim(p, 0).wait_recv()
            rim(p, 1).wait_send()

        inner[p, head_rows, :] = inner[p, head_rows, :] + rim_recv[p, 0].astype(F32)
        inner[p, tail_rows, :] = inner[p, tail_rows, :] + rim_recv[p, 1].astype(F32)
        cols = pl.ds(p * PAIR, PAIR)
        kg_ref[:, cols] = inner[p, :, k_cols].astype(BF16)
        vg_ref[:, cols] = inner[p, :, v_cols].astype(BF16)

    for p in range(pairs - 1):
        collect(p)
    for m in range(1, n_head):
        mix(m).wait()
    acc = mix_send[hme].astype(F32)
    for m in range(1, n_head):
        acc = acc + mix_recv[m - 1].astype(F32)
    mixed_ref[...] = acc.astype(BF16)
    collect(pairs - 1)


def put_out(a0, a1, a2, a3, b0, b1, b2, b3, sem):
    pairs = zip((a0, a1, a2, a3), (b0, b1, b2, b3))
    copies = [pltpu.make_async_copy(a, b, sem.at[i]) for i, (a, b) in enumerate(pairs)]
    for copy in copies:
        copy.start()
    for copy in copies:
        copy.wait()


def body(queries, key_rows, value_rows, out_weight, cotangent):
    frames, feats = queries.shape
    width = out_weight.shape[1]
    n_seq, n_head = lax.axis_size("seq"), lax.axis_size("head")
    plan = Plan(n_seq, frames)
    pairs, wide = feats // PAIR, 2 * PAIR
    units = (frames // BLOCK) * pairs
    keys = 3 * BLOCK + plan.coarse_rows
    share = frames // n_head
    dma = pltpu.SemaphoreType.DMA
    operands = (queries, key_rows, value_rows, out_weight, cotangent)
    shapes = (
        jax.ShapeDtypeStruct((share, width), BF16),
        jax.ShapeDtypeStruct((frames, feats), BF16),
        jax.ShapeDtypeStruct((frames, feats), BF16),
        jax.ShapeDtypeStruct((frames, feats), BF16),
    )
    results = pl.pallas_call(
        functools.partial(kernel, n_seq, n_head, plan),
        out_shape=shapes,
        in_specs=[pl.BlockSpec(memory_space=pltpu.HBM)] * 5,
        out_specs=tuple([pl.BlockSpec(memory_space=pltpu.VMEM)] * 4),
        scratch_shapes=[
            pltpu.VMEM((frames, feats), BF16),
            pltpu.VMEM((pairs, frames + 2 * BLOCK, wide), BF16),
            pltpu.VMEM((feats, width), BF16),
            pltpu.VMEM((frames, width), BF16),
            pltpu.VMEM((pairs, plan.send_rows, wide), BF16),
            pltpu.VMEM((pairs, plan.coarse_rows, wide), BF16),
            pltpu.VMEM((pairs, plan.wide_rows, wide), BF16),
            pltpu.VMEM((frames, feats), BF16),
            pltpu.VMEM((frames, feats), BF16),
            pltpu.VMEM((units, 2 * BLOCK, PAIR), BF16),
            pltpu.VMEM((units, 2 * BLOCK, PAIR), BF16),
            pltpu.VMEM((units, keys, 2 * BLOCK), BF16),
            pltpu.VMEM((units, 1, 2 * BLOCK), F32),
            pltpu.VMEM((n_head, share, width), BF16),
            pltpu.VMEM((max(n_head - 1, 1), share, width), BF16),
            pltpu.VMEM((pairs, 2, BLOCK, wide), BF16),
            pltpu.VMEM((pairs, 2, BLOCK, wide), BF16),
            pltpu.VMEM((pairs, frames, wide), F32),
            pltpu.VMEM((pairs, plan.grad_rows - POOL_ROWS, wide), BF16),
            pltpu.VMEM((pairs, plan.grad_rows, wide), BF16),
            pltpu.VMEM((frames, plan.grad_rows), BF16),
            dma((2 * pairs + 3,)),
            dma((2 * pairs,)),
            dma((2 * pairs,)),
            dma((pairs * (n_seq - 1),)),
            dma((pairs * (n_seq - 1),)),
            dma((2 * pairs,)),
            dma((2 * pairs,)),
            dma((pairs * (n_seq - 1),)),
            dma((pairs * (n_seq - 1),)),
            dma((n_head - 1,)),
            dma((n_head - 1,)),
        ],
        compiler_params=pltpu.CompilerParams(
            collective_id=0, has_side_effects=True, vmem_limit_bytes=32 * 1024 * 1024
        ),
    )(*[pltpu.with_memory_space_constraint(x, pltpu.HBM) for x in operands])
    return pl.pallas_call(
        put_out,
        out_shape=shapes,
        in_specs=[pl.BlockSpec(memory_space=pl.ANY)] * 4,
        out_specs=tuple([pl.BlockSpec(memory_space=pltpu.HBM)] * 4),
        scratch_shapes=[dma((4,))],
        compiler_params=pltpu.CompilerParams(vmem_limit_bytes=1024 * 1024),
    )(*results)


def solution(mesh):
    placed = (P("seq", "head"), P("seq", "head"), P("seq", "head"), P("head", None), P("seq", None))
    return jax.shard_map(
        body,
        mesh=mesh,
        in_specs=placed,
        out_specs=(P(("seq", "head"), None), P("seq", "head"), P("seq", "head"), P("seq", "head")),
        check_vma=False,
    )
```

```python
import functools
import math

import jax
import jax.numpy as jnp
from jax import lax
from jax.experimental import pallas as pl
from jax.experimental.pallas import tpu as pltpu
from jax.sharding import PartitionSpec as P

HEAD_DIM = 64
PAIR = 2 * HEAD_DIM
BLOCK = 128
POOL_ROWS = 64
MIN_SLOT = 16
MASKED = -1000000000.0
MESH = pl.DeviceIdType.MESH
F32 = jnp.float32
BF16 = jnp.bfloat16


def dot_nn(a, b):
    return lax.dot_general(a, b, (((1,), (0,)), ((), ())), preferred_element_type=F32)


def dot_nt(a, b):
    return lax.dot_general(a, b, (((1,), (1,)), ((), ())), preferred_element_type=F32)


def dot_tn(a, b):
    return lax.dot_general(a, b, (((0,), (0,)), ((), ())), preferred_element_type=F32)


class Plan:
    def __init__(self, n_seq, frames):
        self.bits = n_seq.bit_length() - 1
        self.span = frames // POOL_ROWS
        self.rows = [POOL_ROWS >> b for b in range(self.bits)]
        self.slot = [max(MIN_SLOT, r) for r in self.rows]
        self.send_at, at = [], 0
        for b in range(self.bits):
            self.send_at.append(at)
            at += self.slot[b]
        self.send_rows = at
        self.coarse_rows = POOL_ROWS * (1 + self.bits)
        self.direct = [r >= MIN_SLOT for r in self.rows]
        self.wide_at, at = {}, 0
        for b in range(self.bits):
            if not self.direct[b]:
                self.wide_at[b] = at
                at += self.slot[b] << b
        self.wide_rows = max(at, MIN_SLOT)
        self.grad_at, at = {"own": 0}, POOL_ROWS
        for b in range(0, self.bits, 2):
            self.grad_at[b] = at
            at += self.slot[b] << b
        self.even_rows = at
        for b in range(1, self.bits, 2):
            self.grad_at[b] = at
            at += self.slot[b] << b
        self.grad_rows = at


def flip(me, m):
    out, b = me, 0
    while m >> b:
        if (m >> b) & 1:
            out = out + (1 << b) * (1 - 2 * (me // (1 << b) % 2))
        b += 1
    return out


def pool_matrix(plan, frames):
    row = lax.broadcasted_iota(jnp.int32, (plan.send_rows, frames), 0)
    col = lax.broadcasted_iota(jnp.int32, (plan.send_rows, frames), 1)
    hit = None
    for b in range(plan.bits):
        width = plan.span << b
        lo = plan.send_at[b]
        rel = col - (row - lo) * width
        now = (row >= lo) & (row < lo + plan.slot[b]) & (rel >= 0) & (rel < width)
        hit = now if hit is None else hit | now
    return jnp.where(hit, 1.0, 0.0).astype(BF16)


def spread_matrix(plan, frames, levels, base, width_all):
    frame = lax.broadcasted_iota(jnp.int32, (frames, width_all), 0)
    col = lax.broadcasted_iota(jnp.int32, (frames, width_all), 1)
    out = jnp.zeros((frames, width_all), F32)
    for level in levels:
        b = 0 if level == "own" else level
        lo = plan.grad_at[level] - base
        total = POOL_ROWS if level == "own" else plan.slot[b] << b
        width = plan.span << b
        rel = frame - ((col - lo) & (plan.slot[b] - 1)) * width
        hit = (col >= lo) & (col < lo + total) & (rel >= 0) & (rel < width)
        out = jnp.where(hit, 0.5 ** (b // 2), out)
    return out.astype(BF16)


def compact_matrix(plan, b):
    total = plan.slot[b] << b
    row = lax.broadcasted_iota(jnp.int32, (POOL_ROWS, total), 0)
    col = lax.broadcasted_iota(jnp.int32, (POOL_ROWS, total), 1)
    r = plan.rows[b]
    hit = ((col // plan.slot[b]) == (row // r)) & ((col & (plan.slot[b] - 1)) == (row & (r - 1)))
    return jnp.where(hit, 1.0, 0.0).astype(BF16)


def kernel(
    n_seq,
    n_head,
    plan,
    q_hbm,
    k_hbm,
    v_hbm,
    w_hbm,
    c_hbm,
    mixed_ref,
    qg_ref,
    kg_ref,
    vg_ref,
    q_ref,
    ext,
    w_ref,
    c_ref,
    pool_send,
    coarse,
    wide,
    hgrad,
    heads,
    qstack,
    gstack,
    weights,
    delta,
    mix_send,
    mix_recv,
    rim_send,
    rim_recv,
    inner,
    cg_send,
    grad,
    spread,
    load_sem,
    halo_ssem,
    halo_rsem,
    pool_ssem,
    pool_rsem,
    rim_ssem,
    rim_rsem,
    cg_ssem,
    cg_rsem,
    mix_ssem,
    mix_rsem,
):
    me = lax.axis_index("seq")
    hme = lax.axis_index("head")
    frames, feats = q_ref.shape
    blocks = frames // BLOCK
    pairs = feats // PAIR
    bits = plan.bits
    window = 3 * BLOCK
    peers = n_seq - 1

    own_rows = pl.ds(BLOCK, frames)
    k_cols, v_cols = pl.ds(0, PAIR), pl.ds(PAIR, PAIR)
    loads = []
    for p in range(pairs):
        cols = pl.ds(p * PAIR, PAIR)
        for side, (hbm, to) in enumerate(((k_hbm, k_cols), (v_hbm, v_cols))):
            loads.append(
                pltpu.make_async_copy(
                    hbm.at[:, cols], ext.at[p, own_rows, to], load_sem.at[2 * p + side]
                )
            )
    for i, (hbm, ref) in enumerate(((c_hbm, c_ref), (w_hbm, w_ref), (q_hbm, q_ref))):
        loads.append(pltpu.make_async_copy(hbm, ref, load_sem.at[2 * pairs + i]))
    for load in loads:
        load.start()

    barrier = pltpu.get_barrier_semaphore()
    for m in reversed(range(1, n_seq)):
        pl.semaphore_signal(barrier, inc=1, device_id=(flip(me, m), hme), device_id_type=MESH)
    for m in range(1, n_head):
        pl.semaphore_signal(
            barrier, inc=1, device_id=(me, lax.rem(hme + m, n_head)), device_id_type=MESH
        )

    @pl.when(me == 0)
    def _():
        for p in range(pairs):
            ext[p, pl.ds(0, BLOCK), :] = jnp.zeros((BLOCK, 2 * PAIR), BF16)
            rim_recv[p, 0] = jnp.zeros((BLOCK, 2 * PAIR), BF16)

    @pl.when(me == n_seq - 1)
    def _():
        for p in range(pairs):
            ext[p, pl.ds(BLOCK + frames, BLOCK), :] = jnp.zeros((BLOCK, 2 * PAIR), BF16)
            rim_recv[p, 1] = jnp.zeros((BLOCK, 2 * PAIR), BF16)

    pooling = pool_matrix(plan, frames)
    for p in range(pairs):
        loads[2 * p].wait()
        loads[2 * p + 1].wait()
        sums = dot_nn(pooling, ext[p, own_rows, :])
        for b in range(bits):
            at = plan.send_at[b]
            level = sums[at : at + plan.slot[b]] * (1.0 / math.sqrt(plan.span << b))
            pool_send[p, pl.ds(at, plan.slot[b]), :] = level.astype(BF16)
            if b == 0:
                coarse[p, pl.ds(0, POOL_ROWS), :] = level.astype(BF16)

    def halo(p, side):
        return pltpu.make_async_remote_copy(
            src_ref=ext.at[p, pl.ds(frames if side == 0 else BLOCK, BLOCK), :],
            dst_ref=ext.at[p, pl.ds(0 if side == 0 else BLOCK + frames, BLOCK), :],
            send_sem=halo_ssem.at[2 * p + side],
            recv_sem=halo_rsem.at[2 * p + side],
            device_id=(me + 1 if side == 0 else me - 1, hme),
            device_id_type=MESH,
        )

    def panel(p, m):
        b = m.bit_length() - 1
        slot = m - (1 << b)
        if plan.direct[b]:
            at = POOL_ROWS * (1 + b) + slot * plan.slot[b]
            landing = coarse.at[p, pl.ds(at, plan.slot[b]), :]
        else:
            at = plan.wide_at[b] + slot * plan.slot[b]
            landing = wide.at[p, pl.ds(at, plan.slot[b]), :]
        return pltpu.make_async_remote_copy(
            src_ref=pool_send.at[p, pl.ds(plan.send_at[b], plan.slot[b]), :],
            dst_ref=landing,
            send_sem=pool_ssem.at[p * peers + m - 1],
            recv_sem=pool_rsem.at[p * peers + m - 1],
            device_id=(flip(me, m), hme),
            device_id_type=MESH,
        )

    def far_grad(p, m):
        b = m.bit_length() - 1
        at = plan.grad_at[b] + (m - (1 << b)) * plan.slot[b]
        return pltpu.make_async_remote_copy(
            src_ref=cg_send.at[p, pl.ds(at - POOL_ROWS, plan.slot[b]), :],
            dst_ref=grad.at[p, pl.ds(at, plan.slot[b]), :],
            send_sem=cg_ssem.at[p * peers + m - 1],
            recv_sem=cg_rsem.at[p * peers + m - 1],
            device_id=(flip(me, m), hme),
            device_id_type=MESH,
        )

    def rim(p, side):
        return pltpu.make_async_remote_copy(
            src_ref=rim_send.at[p, side],
            dst_ref=rim_recv.at[p, 1 - side],
            send_sem=rim_ssem.at[2 * p + side],
            recv_sem=rim_rsem.at[2 * p + side],
            device_id=(me - 1 if side == 0 else me + 1, hme),
            device_id_type=MESH,
        )

    pl.semaphore_wait(barrier, n_seq - 1 + n_head - 1)

    for p in range(pairs):
        @pl.when(me < n_seq - 1)
        def _():
            halo(p, 0).start()

        @pl.when(me > 0)
        def _():
            halo(p, 1).start()

        for m in reversed(range(1, n_seq)):
            panel(p, m).start()

    for load in loads[2 * pairs :]:
        load.wait()
    hgrad[...] = dot_nt(c_ref[...], w_ref[...]).astype(BF16)

    lane = lax.broadcasted_iota(jnp.int32, (BLOCK, PAIR), 1)
    first = lane < HEAD_DIM

    def stacked(block):
        zero = jnp.zeros_like(block)
        return jnp.concatenate(
            [jnp.where(first, block, zero), jnp.where(first, zero, block)], axis=0
        )

    scale = 1.0 / math.sqrt(HEAD_DIM)
    for p in range(pairs):
        for n in range(blocks):
            u = p * blocks + n
            rows, cols = pl.ds(n * BLOCK, BLOCK), pl.ds(p * PAIR, PAIR)
            qstack[u] = (stacked(q_ref[rows, cols].astype(F32)) * scale).astype(BF16)
            gstack[u] = stacked(hgrad[rows, cols].astype(F32)).astype(BF16)

    even = ["own"] + list(range(0, bits, 2))
    odd = list(range(1, bits, 2))
    spread[:, pl.ds(0, plan.even_rows)] = spread_matrix(plan, frames, even, 0, plan.even_rows)
    odd_rows = plan.grad_rows - plan.even_rows
    if odd:
        spread[:, pl.ds(plan.even_rows, odd_rows)] = spread_matrix(
            plan, frames, odd, plan.even_rows, odd_rows
        )

    left_bias = jnp.where(me == 0, MASKED, 0.0).astype(F32)
    right_bias = jnp.where(me == n_seq - 1, MASKED, 0.0).astype(F32)

    def keys(p, n, cols):
        return ext[p, pl.ds(n * BLOCK, window), cols], coarse[p, :, cols]

    def heads_of(both):
        return jnp.concatenate([both[:HEAD_DIM, :BLOCK], both[HEAD_DIM:, BLOCK:]], axis=0)

    def arrive(p):
        for m in range(1, n_seq):
            panel(p, m).wait()

        @pl.when(me > 0)
        def _():
            halo(p, 0).wait_recv()
            halo(p, 1).wait_send()

        @pl.when(me < n_seq - 1)
        def _():
            halo(p, 1).wait_recv()
            halo(p, 0).wait_send()

        for b in range(bits):
            if not plan.direct[b]:
                packed = wide[p, pl.ds(plan.wide_at[b], plan.slot[b] << b), :]
                coarse[p, pl.ds(POOL_ROWS * (1 + b), POOL_ROWS), :] = dot_nn(
                    compact_matrix(plan, b), packed
                ).astype(BF16)

    def forward(p):
        for n in range(blocks):
            u = p * blocks + n
            rows, cols = pl.ds(n * BLOCK, BLOCK), pl.ds(p * PAIR, PAIR)
            kf, kc = keys(p, n, k_cols)
            vf, vc = keys(p, n, v_cols)
            qs = qstack[u]
            sf = dot_nt(kf, qs)
            sc = dot_nt(kc, qs)
            parts = [sf[i * BLOCK : (i + 1) * BLOCK] for i in range(3)]
            if n == 0:
                parts[0] = parts[0] + left_bias
            if n == blocks - 1:
                parts[2] = parts[2] + right_bias
            parts.append(sc)
            top = functools.reduce(jnp.maximum, [x.max(axis=0, keepdims=True) for x in parts])
            parts = [jnp.exp(x - top) for x in parts]
            total = sum(x.sum(axis=0, keepdims=True) for x in parts)
            inv = 1.0 / total
            parts = [(x * inv).astype(BF16) for x in parts]
            pf = jnp.concatenate(parts[:3], axis=0)
            pc = parts[3]
            weights[u, pl.ds(0, window), :] = pf
            weights[u, pl.ds(window, plan.coarse_rows), :] = pc
            out = heads_of(dot_tn(vf, pf) + dot_tn(vc, pc))
            heads[rows, cols] = out.T.astype(BF16)
            prod = out * hgrad[rows, cols].astype(F32).T
            delta[u] = jnp.concatenate(
                [
                    prod[:HEAD_DIM].sum(axis=0, keepdims=True),
                    prod[HEAD_DIM:].sum(axis=0, keepdims=True),
                ],
                axis=1,
            )

    def backward(p):
        k_parts = [None] * (blocks + 2)
        v_parts = [None] * (blocks + 2)
        k_coarse = v_coarse = None
        for n in range(blocks):
            u = p * blocks + n
            vf, vc = keys(p, n, v_cols)
            qs, gs = qstack[u], gstack[u]
            pf = weights[u, pl.ds(0, window), :]
            pc = weights[u, pl.ds(window, plan.coarse_rows), :]
            dl = delta[u]
            df = (pf.astype(F32) * (dot_nt(vf, gs) - dl)).astype(BF16)
            dc = (pc.astype(F32) * (dot_nt(vc, gs) - dl)).astype(BF16)
            dvf, dvc = dot_nn(pf, gs), dot_nn(pc, gs)
            dkf, dkc = dot_nn(df, qs), dot_nn(dc, qs)
            weights[u, pl.ds(0, window), :] = df
            weights[u, pl.ds(window, plan.coarse_rows), :] = dc
            for i in range(3):
                piece = slice(i * BLOCK, (i + 1) * BLOCK)
                old = k_parts[n + i]
                k_parts[n + i] = dkf[piece] if old is None else old + dkf[piece]
                old = v_parts[n + i]
                v_parts[n + i] = dvf[piece] if old is None else old + dvf[piece]
            k_coarse = dkc if k_coarse is None else k_coarse + dkc
            v_coarse = dvc if v_coarse is None else v_coarse + dvc
        for fine, far, cols in ((k_parts, k_coarse, k_cols), (v_parts, v_coarse, v_cols)):
            rim_send[p, 0, :, cols] = fine[0].astype(BF16)
            rim_send[p, 1, :, cols] = fine[-1].astype(BF16)
            for n in range(blocks):
                inner[p, pl.ds(n * BLOCK, BLOCK), cols] = fine[n + 1]
            far = far.astype(BF16)
            grad[p, pl.ds(0, POOL_ROWS), cols] = far[:POOL_ROWS]
            for b in range(bits):
                level = far[POOL_ROWS * (1 + b) : POOL_ROWS * (2 + b)]
                if not plan.direct[b]:
                    level = dot_tn(compact_matrix(plan, b), level).astype(BF16)
                at = plan.grad_at[b] - POOL_ROWS
                cg_send[p, pl.ds(at, plan.slot[b] << b), cols] = level

        for m in reversed(range(1, n_seq)):
            far_grad(p, m).start()

        @pl.when(me > 0)
        def _():
            rim(p, 0).start()

        @pl.when(me < n_seq - 1)
        def _():
            rim(p, 1).start()

    def query_part(p):
        for n in range(blocks):
            u = p * blocks + n
            rows, cols = pl.ds(n * BLOCK, BLOCK), pl.ds(p * PAIR, PAIR)
            kf, kc = keys(p, n, k_cols)
            df = weights[u, pl.ds(0, window), :]
            dc = weights[u, pl.ds(window, plan.coarse_rows), :]
            dq = heads_of(dot_tn(kf, df) + dot_tn(kc, dc)) * scale
            qg_ref[rows, cols] = dq.T.astype(BF16)

    share = frames // n_head

    def mix(m):
        peer = lax.rem(hme + m, n_head)
        return pltpu.make_async_remote_copy(
            src_ref=mix_send.at[peer],
            dst_ref=mix_recv.at[m - 1],
            send_sem=mix_ssem.at[m - 1],
            recv_sem=mix_rsem.at[m - 1],
            device_id=(me, peer),
            device_id_type=MESH,
        )

    for p in range(pairs):
        arrive(p)
        forward(p)
        if p == pairs - 1:
            mixed = dot_nn(heads[...], w_ref[...]).astype(BF16)
            for h in range(n_head):
                mix_send[h] = mixed[h * share : (h + 1) * share]
            for m in range(1, n_head):
                mix(m).start()
        backward(p)
        query_part(p)

    root = 1.0 / math.sqrt(plan.span)
    head_rows, tail_rows = pl.ds(0, BLOCK), pl.ds(frames - BLOCK, BLOCK)

    def collect(p):
        for m in range(1, n_seq):
            far_grad(p, m).wait()
        total = inner[p] + root * dot_nn(
            spread[:, pl.ds(0, plan.even_rows)], grad[p, pl.ds(0, plan.even_rows), :]
        )
        if odd:
            total = total + (root / math.sqrt(2.0)) * dot_nn(
                spread[:, pl.ds(plan.even_rows, odd_rows)],
                grad[p, pl.ds(plan.even_rows, odd_rows), :],
            )
        inner[p] = total

        @pl.when(me > 0)
        def _():
            rim(p, 1).wait_recv()
            rim(p, 0).wait_send()

        @pl.when(me < n_seq - 1)
        def _():
            rim(p, 0).wait_recv()
            rim(p, 1).wait_send()

        inner[p, head_rows, :] = inner[p, head_rows, :] + rim_recv[p, 0].astype(F32)
        inner[p, tail_rows, :] = inner[p, tail_rows, :] + rim_recv[p, 1].astype(F32)
        cols = pl.ds(p * PAIR, PAIR)
        kg_ref[:, cols] = inner[p, :, k_cols].astype(BF16)
        vg_ref[:, cols] = inner[p, :, v_cols].astype(BF16)

    for p in range(pairs - 1):
        collect(p)
    for m in range(1, n_head):
        mix(m).wait()
    acc = mix_send[hme].astype(F32)
    for m in range(1, n_head):
        acc = acc + mix_recv[m - 1].astype(F32)
    mixed_ref[...] = acc.astype(BF16)
    collect(pairs - 1)


def put_out(a0, a1, a2, a3, b0, b1, b2, b3, sem):
    pairs = zip((a0, a1, a2, a3), (b0, b1, b2, b3))
    copies = [pltpu.make_async_copy(a, b, sem.at[i]) for i, (a, b) in enumerate(pairs)]
    for copy in copies:
        copy.start()
    for copy in copies:
        copy.wait()


def body(queries, key_rows, value_rows, out_weight, cotangent):
    frames, feats = queries.shape
    width = out_weight.shape[1]
    n_seq, n_head = lax.axis_size("seq"), lax.axis_size("head")
    plan = Plan(n_seq, frames)
    pairs, wide = feats // PAIR, 2 * PAIR
    units = (frames // BLOCK) * pairs
    keys = 3 * BLOCK + plan.coarse_rows
    share = frames // n_head
    dma = pltpu.SemaphoreType.DMA
    operands = (queries, key_rows, value_rows, out_weight, cotangent)
    shapes = (
        jax.ShapeDtypeStruct((share, width), BF16),
        jax.ShapeDtypeStruct((frames, feats), BF16),
        jax.ShapeDtypeStruct((frames, feats), BF16),
        jax.ShapeDtypeStruct((frames, feats), BF16),
    )
    results = pl.pallas_call(
        functools.partial(kernel, n_seq, n_head, plan),
        out_shape=shapes,
        in_specs=[pl.BlockSpec(memory_space=pltpu.HBM)] * 5,
        out_specs=tuple([pl.BlockSpec(memory_space=pltpu.VMEM)] * 4),
        scratch_shapes=[
            pltpu.VMEM((frames, feats), BF16),
            pltpu.VMEM((pairs, frames + 2 * BLOCK, wide), BF16),
            pltpu.VMEM((feats, width), BF16),
            pltpu.VMEM((frames, width), BF16),
            pltpu.VMEM((pairs, plan.send_rows, wide), BF16),
            pltpu.VMEM((pairs, plan.coarse_rows, wide), BF16),
            pltpu.VMEM((pairs, plan.wide_rows, wide), BF16),
            pltpu.VMEM((frames, feats), BF16),
            pltpu.VMEM((frames, feats), BF16),
            pltpu.VMEM((units, 2 * BLOCK, PAIR), BF16),
            pltpu.VMEM((units, 2 * BLOCK, PAIR), BF16),
            pltpu.VMEM((units, keys, 2 * BLOCK), BF16),
            pltpu.VMEM((units, 1, 2 * BLOCK), F32),
            pltpu.VMEM((n_head, share, width), BF16),
            pltpu.VMEM((max(n_head - 1, 1), share, width), BF16),
            pltpu.VMEM((pairs, 2, BLOCK, wide), BF16),
            pltpu.VMEM((pairs, 2, BLOCK, wide), BF16),
            pltpu.VMEM((pairs, frames, wide), F32),
            pltpu.VMEM((pairs, plan.grad_rows - POOL_ROWS, wide), BF16),
            pltpu.VMEM((pairs, plan.grad_rows, wide), BF16),
            pltpu.VMEM((frames, plan.grad_rows), BF16),
            dma((2 * pairs + 3,)),
            dma((2 * pairs,)),
            dma((2 * pairs,)),
            dma((pairs * (n_seq - 1),)),
            dma((pairs * (n_seq - 1),)),
            dma((2 * pairs,)),
            dma((2 * pairs,)),
            dma((pairs * (n_seq - 1),)),
            dma((pairs * (n_seq - 1),)),
            dma((n_head - 1,)),
            dma((n_head - 1,)),
        ],
        compiler_params=pltpu.CompilerParams(
            collective_id=0, has_side_effects=True, vmem_limit_bytes=32 * 1024 * 1024
        ),
    )(*[pltpu.with_memory_space_constraint(x, pltpu.HBM) for x in operands])
    return pl.pallas_call(
        put_out,
        out_shape=shapes,
        in_specs=[pl.BlockSpec(memory_space=pl.ANY)] * 4,
        out_specs=tuple([pl.BlockSpec(memory_space=pltpu.HBM)] * 4),
        scratch_shapes=[dma((4,))],
        compiler_params=pltpu.CompilerParams(vmem_limit_bytes=1024 * 1024),
    )(*results)


def solution(mesh):
    placed = (P("seq", "head"), P("seq", "head"), P("seq", "head"), P("head", None), P("seq", None))
    return jax.shard_map(
        body,
        mesh=mesh,
        in_specs=placed,
        out_specs=(P(("seq", "head"), None), P("seq", "head"), P("seq", "head"), P("seq", "head")),
        check_vma=False,
    )
```
